256 devices in a mesh: gx: 32 (over z, x_hi, core), gy: 8 (over x_lo, y).
Axes of the slice: x: 4 (x_hi: 2, x_lo: 2; x = x_hi * 2 + x_lo), y: 4, z: 8, core: 2. Of those that a mesh axis runs over, the one named last changes fastest.
Arguments:
- features: bfloat16 [384, 512, 256], P('gy', 'gx'), may hold values from -6 to 6
- first_filter: bfloat16 [256, 3, 3, 256], P('gy'), may hold values from -0.125 to 0.125
- second_filter: bfloat16 [256, 3, 3, 256], P('gy'), may hold values from -0.125 to 0.125
- cotangent: bfloat16 [256, 512, 384], P('gy', 'gx'), may hold values from -6 to 6
Outputs:
- output: bfloat16 [256, 512, 384], P('gy', 'gx')
- input_grad: bfloat16 [384, 512, 256], P('gy', 'gx')
- first_grad: float32 [256, 3, 3, 256], P('gy')
- second_grad: float32 [256, 3, 3, 256], P('gy')
The draws below stay inside these ranges and needn't reach their ends.
All inputs are finite; a program needn't handle non-finite values.
Results may differ from the reference program's by a relative error of at most 0.0059.
Values may be sent and summed in bfloat16 or wider, within the bound.
A program may use at most 128 MiB of HBM per device.

```python
import math
import jax
import jax.numpy as jnp
from jax import lax

C = 256
ROWS = 384
COLS = 512


def steps_of(rng, shape, shards, low, top_value):
    level = 1.0
    for position, blocks in shards:
        draws = jax.random.uniform(jax.random.fold_in(jax.random.fold_in(rng, 6), position), (blocks,), jnp.float32, low / len(shards), top_value / len(shards))
        level = level * jnp.repeat(jnp.exp(draws), shape[position] // blocks).reshape((-1,) + (1,) * (len(shape) - 1 - position))
    return level


def normal_values(key, shape, scale, most, cuts=(), kind=jnp.bfloat16):
    entries = jax.random.normal(key, shape, jnp.float32) * scale
    if len(cuts) > 0:
        entries = steps_of(key, shape, cuts, -0.22, 0.18) * entries
    return jnp.clip(entries, min=-most, max=most).astype(kind)


def setup_inputs(seed: int = 0) -> dict:
    key_of = jax.random.split(jax.random.key(seed), 5)
    return {
        "features": normal_values(key_of[0], (ROWS, COLS, C), 1.0, 6.0, ((0, 8), (1, 32))),
        "first_filter": normal_values(key_of[1], (C, 3, 3, C), (9 * C) ** -0.5, 0.125, ((0, 8),)),
        "second_filter": normal_values(key_of[2], (C, 3, 3, C), (9 * C) ** -0.5, 0.125, ((0, 8),)),
        "cotangent": normal_values(key_of[3], (C, COLS, ROWS), 1.0, 6.0, ((0, 8), (1, 32))),
    }


def silu_parts(pre):
    sigma = jax.nn.sigmoid(pre)
    return (pre * sigma, sigma * (1.0 + pre * (1.0 - sigma)))

def conv_taps(padded, weight, height, width):
    total = jnp.zeros((height * width, weight.shape[3]), jnp.float32)
    for i in range(3):
        for j in range(3):
            window = padded[i:i + height, j:j + width, :].reshape(height * width, padded.shape[2])
            total = total + jnp.dot(window, weight[i, j], preferred_element_type=jnp.float32)
    return total.reshape(height, width, weight.shape[3])

def flipped(weight):
    return jnp.transpose(weight[::-1, ::-1], (0, 1, 3, 2))

def filter_grad(padded, grad, height, width):
    flat_grad = grad.reshape(height * width, grad.shape[2])
    tap_list = []
    for i in range(3):
        for j in range(3):
            window = padded[i:i + height, j:j + width, :].reshape(height * width, padded.shape[2])
            tap_list.append(lax.dot_general(window, flat_grad, (((0,), (0,)), ((), ())), preferred_element_type=jnp.float32))
    return jnp.stack(tap_list).reshape(3, 3, padded.shape[2], grad.shape[2])

def pad_both(field):
    return jnp.pad(field, ((1, 1), (1, 1), (0, 0)))

def reference(features, first_filter, second_filter, cotangent):
    height = features.shape[0]
    width = features.shape[1]
    scale_factor = 1.0 / math.sqrt(height * width)
    first_taps = jnp.transpose(first_filter, (1, 2, 3, 0))
    second_taps = jnp.transpose(second_filter, (1, 2, 3, 0))
    cot_map = jnp.transpose(cotangent, (2, 1, 0))
    feat_padded = pad_both(features)
    first_pre = conv_taps(feat_padded, first_taps, height, width)
    first_act, first_slope = silu_parts(first_pre)
    hidden = first_act.astype(jnp.bfloat16)
    hidden_padded = pad_both(hidden)
    second_pre = conv_taps(hidden_padded, second_taps, height, width)
    second_act, second_slope = silu_parts(second_pre)
    output = jnp.transpose(second_act.astype(jnp.bfloat16), (2, 1, 0))
    outer_grad = (cot_map.astype(jnp.float32) * second_slope).astype(jnp.bfloat16)
    second_grad = filter_grad(hidden_padded, outer_grad, height, width) * scale_factor
    hidden_grad = conv_taps(pad_both(outer_grad), flipped(second_taps), height, width)
    inner_grad = (hidden_grad * first_slope).astype(jnp.bfloat16)
    first_grad = filter_grad(feat_padded, inner_grad, height, width) * scale_factor
    input_grad = conv_taps(pad_both(inner_grad), flipped(first_taps), height, width).astype(jnp.bfloat16)
    return (output, input_grad, jnp.transpose(first_grad, (3, 0, 1, 2)), jnp.transpose(second_grad, (3, 0, 1, 2)))
```

```python
import functools
import math

import jax
import jax.numpy as jnp
from jax import lax
from jax.experimental import pallas as pl
from jax.experimental.pallas import tpu as pltpu
from jax.sharding import PartitionSpec as P

MESH = pl.DeviceIdType.MESH
F32 = jnp.float32
BF16 = jnp.bfloat16

CH = 256
RB = 48
CB = 16
ST = 64
LANES = 9 * CH
HALF = LANES // 2
PIECE = 384
NGX = 32
NGY = 8

NT = (((1,), (1,)), ((), ()))
NN = (((1,), (0,)), ((), ()))


def mm(a, b, dims):
    return lax.dot_general(a, b, dims, preferred_element_type=F32)


def place(x, y, z, core):
    xw, yw, zw = lax.rem(x + 8, 4), lax.rem(y + 8, 4), lax.rem(z + 16, 8)
    xh = lax.div(xw, 2)
    return {"gx": zw * 4 + xh * 2 + core, "gy": (xw - 2 * xh) * 4 + yw}


def kernel(
    scale,
    feat, w1, w2, cot,
    out_o, ig_o, g1_o, g2_o,
    f32a, p32, fs, pre1, sl1, h32, hs, cott, sendc, sel1, bmat, outs, rout, otb, o32t, o32, os_, i32, imt, is_,
    ig32, amat, sel2, out32, wg, colbuf, rc, rr, t32,
    gf, gb, rb, sb, rx, tz, rz, fin, finp,
    sy, ry, sx, rxs, sc, rcs, sh, rh, scot, rcot, so, ro, sp, rp, spl, rpl, sz, rzs, sg, rg, sf, rf,
):
    gx = lax.axis_index("gx")
    gy = lax.axis_index("gy")
    core = lax.rem(gx, 2)
    xh = lax.rem(lax.div(gx, 2), 2)
    z = lax.div(gx, 4)
    y = lax.rem(gy, 4)
    xl = lax.div(gy, 4)
    x = xh * 2 + xl
    gxl, gxr = lax.rem(gx + NGX - 1, NGX), lax.rem(gx + 1, NGX)
    partner = {"gx": gx + 1 - 2 * core, "gy": gy}

    def at_gy(d, column=None):
        return {"gx": gx if column is None else column, "gy": lax.rem(gy + d, NGY)}

    def rcopy(src, dst, ssem, rsem, dev):
        return pltpu.make_async_remote_copy(
            src_ref=src, dst_ref=dst, send_sem=ssem, recv_sem=rsem, device_id=dev, device_id_type=MESH
        )

    barrier = pltpu.get_barrier_semaphore()
    peers = [at_gy(d) for d in range(1, NGY)]
    peers += [at_gy(d, side) for side in (gxl, gxr) for d in range(NGY)]
    peers += [at_gy(d, z * 4 + (1 - xh) * 2 + core) for d in range(NGY)]
    peers += [place(x + 2 * dxh, y, z + dz, core) for dz in range(1, 8) for dxh in range(2)]
    for peer in peers:
        pl.semaphore_signal(barrier, inc=1, device_id=peer, device_id_type=MESH)
    pl.semaphore_wait(barrier, len(peers))

    pending = []

    def go(copy):
        copy.start()
        pending.append(copy)
        return copy

    filters = (w1, w2)

    def shard_row(xlo, yy):
        return (xlo * 4 + yy) * 32

    ycopies = {}
    xcopies = {}
    ccopies = {}

    def y_send(f, dy):
        row = pl.multiple_of(shard_row(xl, y) + 16 * core, 16)
        src = filters[f].at[pl.ds(pl.multiple_of(16 * core, 16), 16), :]
        ycopies[f, dy] = go(
            rcopy(src, wg.at[f, pl.ds(row, 16), :], sy.at[f, dy - 1], ry.at[f, dy - 1], place(x, y + dy, z, core))
        )

    def x_send(f, dy):
        row = pl.multiple_of(shard_row(xl, lax.rem(y - dy + 4, 4)) + 16 * core, 16)
        for side in range(2):
            if dy == 0:
                src = filters[f].at[pl.ds(pl.multiple_of(16 * core, 16), 16), pl.ds(side * HALF, HALF)]
            else:
                src = wg.at[f, pl.ds(row, 16), pl.ds(side * HALF, HALF)]
            dst = wg.at[f, pl.ds(row, 16), pl.ds(side * HALF, HALF)]
            xcopies[f, dy, side] = go(
                rcopy(src, dst, sx.at[f, dy, side], rxs.at[f, dy, side], place(x + 1 - 2 * side, y, z, core))
            )

    def c_send(f, other, dy):
        xlo = 1 - xl if other else xl
        row = pl.multiple_of(shard_row(xlo, lax.rem(y - dy + 4, 4)) + 16 * core, 16)
        ref = wg.at[f, pl.ds(row, 16), :]
        ccopies[f, other, dy] = go(rcopy(ref, ref, sc.at[f, other, dy], rcs.at[f, other, dy], partner))

    def filter_start(f):
        for dy in (1, 3, 2):
            y_send(f, dy)
        x_send(f, 0)
        wg[f, pl.ds(pl.multiple_of(shard_row(xl, y), 32), 32), :] = filters[f][...]

    def filter_pass(f):
        for dy in (1, 3, 2):
            ycopies[f, dy].wait_recv()
            x_send(f, dy)
            c_send(f, 0, dy)
        for dy in (0, 1, 3, 2):
            for side in range(2):
                xcopies[f, dy, side].wait_recv()
            c_send(f, 1, dy)

    def filter_end(f):
        for dy in (1, 3, 2):
            ccopies[f, 0, dy].wait_recv()
        for dy in (0, 1, 3, 2):
            ccopies[f, 1, dy].wait_recv()

    def split(ref, value):
        for k in range(value.shape[1] // 128):
            ref[k] = value[:, k * 128:(k + 1) * 128]

    def strided(ref, start, size, stride):
        return jnp.concatenate([ref[k, pl.ds(start, size, stride=stride), :] for k in range(ref.shape[0])], axis=1)

    def put_strided(ref, start, size, stride, value):
        for k in range(ref.shape[0]):
            ref[k, pl.ds(start, size, stride=stride), :] = value[:, k * 128:(k + 1) * 128]

    def joined(ref):
        return jnp.concatenate([ref[k] for k in range(ref.shape[0])], axis=1)

    filter_start(0)

    hcopies = []
    for v, (rows, dg) in enumerate(((RB - 4, 1), (0, NGY - 1))):
        for h, column in enumerate((gxr, None, gxl)):
            hcopies.append(
                go(rcopy(feat.at[pl.ds(rows, 4)], rr.at[v, h], sh.at[v, h], rh.at[v, h], at_gy(dg, column)))
            )
    split(f32a, feat[...].astype(F32).reshape(RB * CB, CH))
    for c in (12, 13, 14, 15, 0, 1, 2, 3):
        colbuf[0 if c > 7 else 1, c % 4] = strided(f32a, c, RB, CB).astype(BF16)
    hcopies.append(go(rcopy(colbuf.at[0], rc.at[0], sh.at[2, 0], rh.at[2, 0], at_gy(0, gxr))))
    hcopies.append(go(rcopy(colbuf.at[1], rc.at[1], sh.at[2, 1], rh.at[2, 1], at_gy(0, gxl))))

    filter_start(1)

    split(out32, cot[...].astype(F32).reshape(32 * CB, 384))
    for c in range(CB):
        bmat[pl.ds((c // 2) * 32, 32), pl.ds((c % 2) * 384, 384)] = strided(out32, c, 32, CB).astype(BF16)
    rows_k = lax.broadcasted_iota(jnp.int32, (768, 128), 0)
    lane = lax.broadcasted_iota(jnp.int32, (1, 128), 1)
    high = jnp.where(lane >= 64, 1, 0)
    for b in range(NGY):
        row_of = 48 * b - 8 + lane - 64 * high
        target = jnp.where((row_of >= 0) & (row_of < 384), row_of + 384 * high, -1)
        sel1[...] = jnp.where(rows_k == target, 1.0, 0.0).astype(BF16)
        res = mm(bmat[...], sel1[...], NN).astype(BF16)
        for cp in range(8):
            sendc[b, :, pl.ds(cp * 128, 128)] = res[cp * 32:(cp + 1) * 32, :]
    row = pl.multiple_of(gy * 32, 32)
    cotcopies = []
    for d in range(1, NGY):
        dev = at_gy(d)
        cotcopies.append(
            go(rcopy(sendc.at[dev["gy"]], cott.at[pl.ds(row, 32), pl.ds(128, 1024)], scot.at[0, d], rcot.at[0, d], dev))
        )
    for d in range(NGY):
        for side, column in ((1, gxr), (2, gxl)):
            dev = at_gy(d, column)
            src = sendc.at[dev["gy"], :, pl.ds(896 if side == 1 else 0, 128)]
            dst = cott.at[pl.ds(row, 32), pl.ds(0 if side == 1 else 1152, 128)]
            cotcopies.append(go(rcopy(src, dst, scot.at[side, d], rcot.at[side, d], dev)))
    cott[pl.ds(row, 32), pl.ds(128, 1024)] = sendc[gy]

    filter_pass(0)

    p32[...] = jnp.zeros_like(p32)
    for c in range(CB):
        p32[pl.ds(8 + (4 + c) * ST + 8, RB), :] = strided(f32a, c, RB, CB)
    for copy in hcopies:
        copy.wait_recv()
    in_left = jnp.where(gx > 0, 1.0, 0.0)
    in_right = jnp.where(gx < NGX - 1, 1.0, 0.0)
    in_up = jnp.where(gy > 0, 1.0, 0.0)
    in_down = jnp.where(gy < NGY - 1, 1.0, 0.0)
    for c in range(4):
        p32[pl.ds(8 + c * ST + 8, RB), :] = rc[0, c].astype(F32) * in_left
        p32[pl.ds(8 + (20 + c) * ST + 8, RB), :] = rc[1, c].astype(F32) * in_right
    for v, in_v in enumerate((in_up, in_down)):
        for h, in_h in enumerate((in_left, 1.0, in_right)):
            split(t32.at[v, h], rr[v, h].astype(F32).reshape(64, CH) * (in_v * in_h))
            for c in range(CB):
                col = (c - 12, c + 4, c + 20)[h]
                if 0 <= col < 24:
                    p32[pl.ds(8 + col * ST + (4 if v == 0 else 56), 4), :] = strided(t32.at[v, h], c, 4, CB)

    def shifts(src, dst, count):
        for d in range(3):
            dst[:, pl.ds(d * CH, CH)] = src[pl.ds(7 + d, count), :].astype(BF16)

    shifts(p32, fs, 24 * ST)
    filter_end(0)

    def tap(f, i, j):
        return wg[f, :, pl.ds((i * 3 + j) * CH, CH)]

    def taps_in(f, j):
        return jnp.concatenate([tap(f, i, j) for i in range(3)], axis=1)

    def taps_out(f, j):
        return jnp.concatenate([tap(f, 2 - i, j) for i in range(3)], axis=0)

    for t in range(2):
        acc = None
        for j in range(3):
            term = mm(fs[pl.ds(j * ST + t * 704, 704), :], taps_in(0, j), NT)
            acc = term if acc is None else acc + term
        pre1[pl.ds(t * 704, 704), :] = acc

    filter_pass(1)

    row_in = lax.broadcasted_iota(jnp.int32, (ST, CH), 0) + (48 * gy - 8)
    rows_ok = (row_in >= 0) & (row_in < 384)
    rows_ok_f = jnp.where(rows_ok, 1.0, 0.0)
    h32[pl.ds(0, 8), :] = jnp.zeros((8, CH), F32)
    h32[pl.ds(8 + 22 * ST, 8), :] = jnp.zeros((8, CH), F32)

    @pl.loop(0, 22)
    def _(c):
        at = pl.multiple_of(c * ST, ST)
        v = pre1[pl.ds(at, ST), :]
        s = 1.0 / (1.0 + jnp.exp(-v))
        col = 16 * gx + c - 3
        ok = jnp.where((col >= 0) & (col < 512), 1.0, 0.0)
        h32[pl.ds(at + 8, ST), :] = v * s * (rows_ok_f * ok)
        sl1[pl.ds(at, ST), :] = s * (1.0 + v * (1.0 - s))

    shifts(h32, hs, 22 * ST)
    filter_end(1)
    for copy in cotcopies:
        copy.wait_recv()

    lane2 = lax.broadcasted_iota(jnp.int32, (CH, 256), 1)
    in_block = jnp.where(((lane2 & 63) >= 8) & ((lane2 & 63) < 56), 1.0, 0.0)
    for t in range(5):
        acc = None
        for j in range(3):
            term = mm(taps_in(1, j), hs[pl.ds(j * ST + t * 256, 256), :], NT)
            acc = term if acc is None else acc + term
        s = 1.0 / (1.0 + jnp.exp(-acc))
        act = (acc * s).astype(BF16).reshape(NGY, 32, 256)
        outer = cott[:, pl.ds(t * 256, 256)].astype(F32) * (s * (1.0 + acc * (1.0 - s)))
        if t == 0:
            outer = jnp.where((lane2 >= 128) | (gx > 0), outer, 0.0)
        if t == 4:
            outer = jnp.where((lane2 < 128) | (gx < NGX - 1), outer, 0.0)
        o32t[:, pl.ds(t * 256, 256)] = outer
        own = (outer * in_block).astype(BF16)
        lo, hi = (128 if t == 0 else 0), (128 if t == 4 else 256)
        outs[:, :, pl.ds(t * 256 + lo - 128, hi - lo)] = act[:, :, lo:hi]
        otb[:, pl.ds(t * 256 + lo - 128, hi - lo)] = own[:, lo:hi]

    outcopies = []
    for d in range(1, NGY):
        dev = at_gy(d)
        outcopies.append(go(rcopy(outs.at[dev["gy"]], rout.at[gy], so.at[d], ro.at[d], dev)))
    rout[gy] = outs[gy]

    def grad(g, left, right, base):
        for j in range(3):
            part = mm(left[...], right[pl.ds((base + j) * ST, 1024), :], NN)
            for i in range(3):
                value = part[:, i * CH:(i + 1) * CH].reshape(8, 2, 16, CH)
                gf[g, :, :, :, pl.ds((i * 3 + j) * CH, CH)] = value
                gb[g, :, :, :, pl.ds((i * 3 + j) * CH, CH)] = value.astype(BF16)
        return go(rcopy(gb.at[g, :, 1 - core], rb.at[g], sp.at[g], rp.at[g], partner))

    def plane(g, pair):
        pair.wait_recv()

        @pl.loop(0, NGY)
        def _(b):
            for k in range(2):
                part = gf[g, b, core, :, pl.ds(k * HALF, HALF)] + rb[g, b, :, pl.ds(k * HALF, HALF)].astype(F32)
                sb[g, b, k] = part.astype(BF16)

        copies = []
        for dx, dy in ((1, 0), (3, 0), (0, 1), (0, 3), (1, 1), (3, 3), (1, 3), (3, 1), (2, 0), (0, 2), (2, 1), (1, 2), (2, 3), (3, 2), (2, 2)):
            tx = lax.rem(x + dx, 4)
            dev = place(x + dx, y + dy, z, core)
            slot = dx * 4 + dy
            copies.append(
                go(rcopy(sb.at[g, dev["gy"], lax.div(tx, 2)], rx.at[g, slot], spl.at[g, slot], rpl.at[g, slot], dev))
            )
        return copies

    pair2 = grad(1, otb, hs, 2)

    o32[pl.ds(0, 8), :] = jnp.zeros((8, CH), F32)
    o32[pl.ds(8 + 20 * ST, 8), :] = jnp.zeros((8, CH), F32)
    for t in range(5):
        o32[pl.ds(8 + t * 256, 256), :] = o32t[:, pl.ds(t * 256, 256)].T
    shifts(o32, os_, 20 * ST)

    plane2 = plane(1, pair2)

    i32[pl.ds(0, 8), :] = jnp.zeros((8, CH), F32)
    i32[pl.ds(8 + 18 * ST, 8), :] = jnp.zeros((8, CH), F32)
    for t in range(2):
        acc = None
        for j in range(3):
            term = mm(os_[pl.ds((2 - j) * ST + t * 576, 576), :], taps_out(1, j), NN)
            acc = term if acc is None else acc + term
        i32[pl.ds(8 + t * 576, 576), :] = acc

    @pl.loop(0, 18)
    def _(c):
        at = pl.multiple_of(c * ST, ST)
        col = 16 * gx + c - 1
        ok = jnp.where((col >= 0) & (col < 512), 1.0, 0.0)
        i32[pl.ds(at + 8, ST), :] = i32[pl.ds(at + 8, ST), :] * sl1[pl.ds(at + 128, ST), :] * (rows_ok_f * ok)

    for t in range(4):
        imt[:, pl.ds(t * 256, 256)] = (i32[pl.ds(8 + 64 + t * 256, 256), :].T * in_block).astype(BF16)
    pair1 = grad(0, imt, fs, 3)

    shifts(i32, is_, 18 * ST)
    plane1 = plane(0, pair1)
    acc = None
    for j in range(3):
        term = mm(is_[pl.ds((2 - j) * ST, 1024), :], taps_out(0, j), NN)
        acc = term if acc is None else acc + term
    for c in range(CB):
        put_strided(ig32, c, RB, CB, acc[c * ST + 8:c * ST + 8 + RB, :])
    ig_o[...] = joined(ig32).astype(BF16).reshape(RB, CB, CH)

    for copy in outcopies:
        copy.wait_recv()
    rows_n = lax.broadcasted_iota(jnp.int32, (1024, 384), 0)
    h_lane = lax.broadcasted_iota(jnp.int32, (1, 384), 1)
    band = jnp.zeros((1, 384), jnp.int32)
    for b in range(1, NGY):
        band = band + jnp.where(h_lane >= 48 * b, 1, 0)
    for src in range(NGY):
        for cp in range(8):
            amat[pl.ds(cp * 32, 32), pl.ds(src * 128, 128)] = rout[src, :, pl.ds(cp * 128, 128)]
    for par in range(2):
        target = band * 80 + h_lane + (8 + 64 * par)
        sel2[...] = jnp.where(rows_n == target, 1.0, 0.0).astype(BF16)
        res = mm(amat[...], sel2[...], NN)
        for cp in range(8):
            put_strided(out32, 2 * cp + par, 32, CB, res[cp * 32:(cp + 1) * 32, :])
    out_o[...] = joined(out32).astype(BF16).reshape(32, CB, 384)

    for g, copies in ((1, plane2), (0, plane1)):
        for copy in copies:
            copy.wait_recv()
        for k in range(3):
            lanes = pl.ds(k * PIECE, PIECE)
            total = sb[g, gy, xh, :, lanes].astype(F32)
            for slot in range(1, 16):
                total = total + rx[g, slot, :, lanes].astype(F32)
            tz[g * 3 + k] = total.astype(BF16)
    tz[pl.ds(6, 2)] = jnp.zeros((2, 16, PIECE), BF16)
    zcopies = []
    for dz in (1, 7, 2, 6, 3, 5, 4):
        zt = lax.rem(z + dz, 8)
        zcopies.append(go(rcopy(tz.at[zt], rz.at[dz], sz.at[dz], rzs.at[dz], place(x, y, z + dz, core))))
    for copy in zcopies:
        copy.wait_recv()
    total = tz[z].astype(F32)
    for dz in range(1, 8):
        total = total + rz[dz].astype(F32)
    slot = z * 2 + xh
    fin[slot] = total.astype(BF16)
    gcopies = []
    for dz in range(8):
        for dxh in range(2):
            if dz or dxh:
                gcopies.append(
                    go(rcopy(fin.at[slot], fin.at[slot], sg.at[dz, dxh], rg.at[dz, dxh], place(x + 2 * dxh, y, z + dz, core)))
                )
    for copy in gcopies:
        copy.wait_recv()
    last = go(rcopy(fin.at[pl.ds(0, 12)], finp, sf, rf, partner))
    mine = pl.multiple_of(16 * core, 16)
    theirs = pl.multiple_of(16 - 16 * core, 16)
    outs_g = (g1_o, g2_o)
    for q in range(12):
        lanes = pl.ds((q % 2) * HALF + ((q // 2) % 3) * PIECE, PIECE)
        outs_g[q // 6][pl.ds(mine, 16), lanes] = fin[q].astype(F32) * scale
    last.wait_recv()
    for q in range(12):
        lanes = pl.ds((q % 2) * HALF + ((q // 2) % 3) * PIECE, PIECE)
        outs_g[q // 6][pl.ds(theirs, 16), lanes] = finp[q].astype(F32) * scale
    for copy in pending:
        copy.wait_send()


def solution(mesh):
    scale = 1.0 / math.sqrt(384 * 512)
    vm = pltpu.VMEM
    dma = pltpu.SemaphoreType.DMA
    scratch = [
        vm((2, 768, 128), F32),
        vm((24 * ST + 16, CH), F32),
        vm((24 * ST, 768), BF16),
        vm((22 * ST, CH), F32),
        vm((22 * ST, CH), F32),
        vm((22 * ST + 16, CH), F32),
        vm((22 * ST, 768), BF16),
        vm((CH, 1280), BF16),
        vm((8, 32, 1024), BF16),
        vm((768, 128), BF16),
        vm((256, 768), BF16),
        vm((8, 32, 1024), BF16),
        vm((8, 32, 1024), BF16),
        vm((CH, 1024), BF16),
        vm((CH, 1280), F32),
        vm((20 * ST + 16, CH), F32),
        vm((20 * ST, 768), BF16),
        vm((18 * ST + 16, CH), F32),
        vm((CH, 1024), BF16),
        vm((18 * ST, 768), BF16),
        vm((2, 768, 128), F32),
        vm((256, 1024), BF16),
        vm((1024, 384), BF16),
        vm((3, 512, 128), F32),
        vm((2, CH, LANES), BF16),
        vm((2, 4, RB, CH), BF16),
        vm((2, 4, RB, CH), BF16),
        vm((2, 3, 4, 16, CH), BF16),
        vm((2, 3, 2, 64, 128), F32),
        vm((2, 8, 2, 16, LANES), F32),
        vm((2, 8, 2, 16, LANES), BF16),
        vm((2, 8, 16, LANES), BF16),
        vm((2, 8, 2, 16, HALF), BF16),
        vm((2, 16, 16, HALF), BF16),
        vm((8, 16, PIECE), BF16),
        vm((8, 16, PIECE), BF16),
        vm((16, 16, PIECE), BF16),
        vm((12, 16, PIECE), BF16),
        dma((2, 3)), dma((2, 3)),
        dma((2, 4, 2)), dma((2, 4, 2)),
        dma((2, 2, 4)), dma((2, 2, 4)),
        dma((3, 3)), dma((3, 3)),
        dma((3, 8)), dma((3, 8)),
        dma((8,)), dma((8,)),
        dma((2,)), dma((2,)),
        dma((2, 16)), dma((2, 16)),
        dma((8,)), dma((8,)),
        dma((8, 2)), dma((8, 2)),
        dma, dma,
    ]
    call = pl.pallas_call(
        functools.partial(kernel, scale),
        name="step",
        out_shape=(
            jax.ShapeDtypeStruct((32, CB, 384), BF16),
            jax.ShapeDtypeStruct((RB, CB, CH), BF16),
            jax.ShapeDtypeStruct((32, LANES), F32),
            jax.ShapeDtypeStruct((32, LANES), F32),
        ),
        in_specs=[pl.BlockSpec(memory_space=pltpu.VMEM)] * 4,
        out_specs=[pl.BlockSpec(memory_space=pltpu.VMEM)] * 4,
        scratch_shapes=scratch,
        compiler_params=pltpu.CompilerParams(
            collective_id=0, has_side_effects=True, vmem_limit_bytes=60 * 1024 * 1024
        ),
    )

    def body(features, first_filter, second_filter, cotangent):
        out, ig, g1, g2 = call(
            features, first_filter.reshape(32, LANES), second_filter.reshape(32, LANES), cotangent
        )
        return out, ig, g1.reshape(32, 3, 3, CH), g2.reshape(32, 3, 3, CH)

    in_specs = (
        P("gy", "gx", None),
        P("gy", None, None, None),
        P("gy", None, None, None),
        P("gy", "gx", None),
    )
    out_specs = (
        P("gy", "gx", None),
        P("gy", "gx", None),
        P("gy", None, None, None),
        P("gy", None, None, None),
    )
    return jax.shard_map(body, mesh=mesh, in_specs=in_specs, out_specs=out_specs, check_vma=False)
```

```python
import functools
import math

import jax
import jax.numpy as jnp
from jax import lax
from jax.experimental import pallas as pl
from jax.experimental.pallas import tpu as pltpu
from jax.sharding import PartitionSpec as P

MESH = pl.DeviceIdType.MESH
F32 = jnp.float32
BF16 = jnp.bfloat16

CH = 256
RB = 48
CB = 16
ST = 64
OWNERS = 5
NGX = 32
NGY = 8

NT = (((1,), (1,)), ((), ()))
NN = (((1,), (0,)), ((), ()))


def mm(a, b, dims):
    return lax.dot_general(a, b, dims, preferred_element_type=F32)


def place(x, y, z, core):
    xw, yw, zw = lax.rem(x + 8, 4), lax.rem(y + 8, 4), lax.rem(z + 16, 8)
    xh = lax.div(xw, 2)
    return {"gx": zw * 4 + xh * 2 + core, "gy": (xw - 2 * xh) * 4 + yw}


def kernel(
    scale,
    feat_i, w1_i, w2_i, cot_i,
    out_o, ig_o, g1_o, g2_o,
    feat, w1, w2, cot, outv, igv, gv,
    f32a, p32, fs, pre1, sl1, h32, hs, cott, sendc, sel1, bmat, outs, rout, otb, o32t, o32, os_, i32, imt, is_,
    ig32, amat, sel2, out32, wg, colbuf, rc, rr, t32,
    gf, gb, rb, sb, rx, tz, rz, fin, finp,
    sy, ry, sx, rxs, sc, rcs, sh, rh, scot, rcot, so, ro, sp, rp, spl, rpl, sz, rzs, sg, rg, sf, rf, sin, sout,
):
    gx = lax.axis_index("gx")
    gy = lax.axis_index("gy")
    core = lax.rem(gx, 2)
    xh = lax.rem(lax.div(gx, 2), 2)
    z = lax.div(gx, 4)
    y = lax.rem(gy, 4)
    xl = lax.div(gy, 4)
    x = xh * 2 + xl
    gxl, gxr = lax.rem(gx + NGX - 1, NGX), lax.rem(gx + 1, NGX)
    partner = {"gx": gx + 1 - 2 * core, "gy": gy}

    def at_gy(d, column=None):
        return {"gx": gx if column is None else column, "gy": lax.rem(gy + d, NGY)}

    def rcopy(src, dst, ssem, rsem, dev):
        return pltpu.make_async_remote_copy(
            src_ref=src, dst_ref=dst, send_sem=ssem, recv_sem=rsem, device_id=dev, device_id_type=MESH
        )

    loads = [
        pltpu.make_async_copy(src, dst, sin.at[n])
        for n, (src, dst) in enumerate(((w1_i, w1), (feat_i, feat), (w2_i, w2), (cot_i, cot)))
    ]
    for load in loads:
        load.start()

    barrier = pltpu.get_barrier_semaphore()
    peers = [at_gy(d) for d in range(1, NGY)]
    peers += [at_gy(d, side) for side in (gxl, gxr) for d in range(NGY)]
    peers += [at_gy(d, z * 4 + (1 - xh) * 2 + core) for d in range(NGY)]
    peers += [place(x + 2 * dxh, y, z + dz, core) for dz in range(1, 8) for dxh in range(2)]
    for peer in peers:
        pl.semaphore_signal(barrier, inc=1, device_id=peer, device_id_type=MESH)
    pl.semaphore_wait(barrier, len(peers))
    loads[0].wait()

    pending = []

    def go(copy):
        copy.start()
        pending.append(copy)
        return copy

    filters = (w1, w2)

    def shard_row(xlo, yy):
        return (xlo * 4 + yy) * 32

    ycopies = {}
    xcopies = {}
    ccopies = {}

    def y_send(f, dy):
        row = pl.multiple_of(shard_row(xl, y) + 16 * core, 16)
        src = filters[f].at[:, pl.ds(pl.multiple_of(16 * core, 16), 16), :]
        ycopies[f, dy] = go(
            rcopy(src, wg.at[f, :, pl.ds(row, 16), :], sy.at[f, dy - 1], ry.at[f, dy - 1], place(x, y + dy, z, core))
        )

    def x_send(f, dy):
        row = pl.multiple_of(shard_row(xl, lax.rem(y - dy + 4, 4)) + 16 * core, 16)
        for side in range(2):
            lanes = pl.ds(side * 128, 128)
            if dy == 0:
                src = filters[f].at[:, pl.ds(pl.multiple_of(16 * core, 16), 16), lanes]
            else:
                src = wg.at[f, :, pl.ds(row, 16), lanes]
            dst = wg.at[f, :, pl.ds(row, 16), lanes]
            xcopies[f, dy, side] = go(
                rcopy(src, dst, sx.at[f, dy, side], rxs.at[f, dy, side], place(x + 1 - 2 * side, y, z, core))
            )

    def c_send(f, other, dy):
        xlo = 1 - xl if other else xl
        row = pl.multiple_of(shard_row(xlo, lax.rem(y - dy + 4, 4)) + 16 * core, 16)
        ref = wg.at[f, :, pl.ds(row, 16), :]
        ccopies[f, other, dy] = go(rcopy(ref, ref, sc.at[f, other, dy], rcs.at[f, other, dy], partner))

    def own_shard(f):
        wg[f, :, pl.ds(pl.multiple_of(shard_row(xl, y), 32), 32), :] = filters[f][...]

    def filter_y(f):
        for dy in (1, 3, 2):
            y_send(f, dy)

    def filter_relay(f, dy):
        ycopies[f, dy].wait_recv()
        x_send(f, dy)
        c_send(f, 0, dy)

    def filter_swap(f):
        for dy in (0, 1, 3, 2):
            for side in range(2):
                xcopies[f, dy, side].wait_recv()
            c_send(f, 1, dy)

    def filter_end(f):
        for dy in (1, 3, 2):
            ccopies[f, 0, dy].wait_recv()
        for dy in (0, 1, 3, 2):
            ccopies[f, 1, dy].wait_recv()

    def split(ref, value):
        for k in range(value.shape[1] // 128):
            ref[k] = value[:, k * 128:(k + 1) * 128]

    def strided(ref, start, size, stride):
        return jnp.concatenate([ref[k, pl.ds(start, size, stride=stride), :] for k in range(ref.shape[0])], axis=1)

    def put_strided(ref, start, size, stride, value):
        for k in range(ref.shape[0]):
            ref[k, pl.ds(start, size, stride=stride), :] = value[:, k * 128:(k + 1) * 128]

    def joined(ref):
        return jnp.concatenate([ref[k] for k in range(ref.shape[0])], axis=1)

    filter_y(0)
    x_send(0, 0)
    loads[1].wait()

    hcopies = []
    for v, (rows, dg) in enumerate(((RB - 4, 1), (0, NGY - 1))):
        for h, column in enumerate((gxr, None, gxl)):
            hcopies.append(
                go(rcopy(feat.at[pl.ds(rows, 4)], rr.at[v, h], sh.at[v, h], rh.at[v, h], at_gy(dg, column)))
            )
    split(f32a, feat[...].astype(F32).reshape(RB * CB, CH))
    for c in (12, 13, 14, 15, 0, 1, 2, 3):
        colbuf[0 if c > 7 else 1, c % 4] = strided(f32a, c, RB, CB).astype(BF16)
    hcopies.append(go(rcopy(colbuf.at[0], rc.at[0], sh.at[2, 0], rh.at[2, 0], at_gy(0, gxr))))
    hcopies.append(go(rcopy(colbuf.at[1], rc.at[1], sh.at[2, 1], rh.at[2, 1], at_gy(0, gxl))))

    loads[2].wait()
    filter_y(1)
    own_shard(0)
    own_shard(1)
    loads[3].wait()

    split(out32, cot[...].astype(F32).reshape(32 * CB, 384))
    for c in range(CB):
        bmat[pl.ds((c // 2) * 32, 32), pl.ds((c % 2) * 384, 384)] = strided(out32, c, 32, CB).astype(BF16)
    rows_k = lax.broadcasted_iota(jnp.int32, (768, 128), 0)
    lane = lax.broadcasted_iota(jnp.int32, (1, 128), 1)
    high = jnp.where(lane >= 64, 1, 0)

    def cot_rows(b):
        row_of = 48 * b - 8 + lane - 64 * high
        target = jnp.where((row_of >= 0) & (row_of < 384), row_of + 384 * high, -1)
        sel1[...] = jnp.where(rows_k == target, 1.0, 0.0).astype(BF16)
        res = mm(bmat[...], sel1[...], NN).astype(BF16)
        for cp in range(8):
            sendc[b, :, pl.ds(cp * 128, 128)] = res[cp * 32:(cp + 1) * 32, :]

    filter_relay(0, 1)
    filter_relay(0, 3)
    for b in range(4):
        cot_rows(b)
    filter_relay(0, 2)
    for b in range(4, NGY):
        cot_rows(b)
    filter_swap(0)
    x_send(1, 0)
    for dy in (1, 3, 2):
        filter_relay(1, dy)

    row = pl.multiple_of(gy * 32, 32)
    cotcopies = []
    for d in range(1, NGY):
        dev = at_gy(d)
        cotcopies.append(
            go(rcopy(sendc.at[dev["gy"]], cott.at[pl.ds(row, 32), pl.ds(128, 1024)], scot.at[0, d], rcot.at[0, d], dev))
        )
    for d in range(NGY):
        for side, column in ((1, gxr), (2, gxl)):
            dev = at_gy(d, column)
            src = sendc.at[dev["gy"], :, pl.ds(896 if side == 1 else 0, 128)]
            dst = cott.at[pl.ds(row, 32), pl.ds(0 if side == 1 else 1152, 128)]
            cotcopies.append(go(rcopy(src, dst, scot.at[side, d], rcot.at[side, d], dev)))
    cott[pl.ds(row, 32), pl.ds(128, 1024)] = sendc[gy]

    p32[...] = jnp.zeros_like(p32)
    for c in range(CB):
        p32[pl.ds(8 + (4 + c) * ST + 8, RB), :] = strided(f32a, c, RB, CB)
    for copy in hcopies:
        copy.wait_recv()
    in_left = jnp.where(gx > 0, 1.0, 0.0)
    in_right = jnp.where(gx < NGX - 1, 1.0, 0.0)
    in_up = jnp.where(gy > 0, 1.0, 0.0)
    in_down = jnp.where(gy < NGY - 1, 1.0, 0.0)
    for c in range(4):
        p32[pl.ds(8 + c * ST + 8, RB), :] = rc[0, c].astype(F32) * in_left
        p32[pl.ds(8 + (20 + c) * ST + 8, RB), :] = rc[1, c].astype(F32) * in_right
    for v, in_v in enumerate((in_up, in_down)):
        for h, in_h in enumerate((in_left, 1.0, in_right)):
            split(t32.at[v, h], rr[v, h].astype(F32).reshape(64, CH) * (in_v * in_h))
            for c in range(CB):
                col = (c - 12, c + 4, c + 20)[h]
                if 0 <= col < 24:
                    p32[pl.ds(8 + col * ST + (4 if v == 0 else 56), 4), :] = strided(t32.at[v, h], c, 4, CB)

    def shifts(src, dst, count):
        for d in range(3):
            dst[:, pl.ds(d * CH, CH)] = src[pl.ds(7 + d, count), :].astype(BF16)

    shifts(p32, fs, 24 * ST)
    filter_end(0)

    def tap(f, i, j):
        return wg[f, i * 3 + j]

    def taps_in(f, j):
        return jnp.concatenate([tap(f, i, j) for i in range(3)], axis=1)

    def taps_out(f, j):
        return jnp.concatenate([tap(f, 2 - i, j) for i in range(3)], axis=0)

    for t in range(2):
        acc = None
        for j in range(3):
            term = mm(fs[pl.ds(j * ST + t * 704, 704), :], taps_in(0, j), NT)
            acc = term if acc is None else acc + term
        pre1[pl.ds(t * 704, 704), :] = acc

    filter_swap(1)

    row_in = lax.broadcasted_iota(jnp.int32, (ST, CH), 0) + (48 * gy - 8)
    rows_ok = (row_in >= 0) & (row_in < 384)
    rows_ok_f = jnp.where(rows_ok, 1.0, 0.0)
    h32[pl.ds(0, 8), :] = jnp.zeros((8, CH), F32)
    h32[pl.ds(8 + 22 * ST, 8), :] = jnp.zeros((8, CH), F32)

    @pl.loop(0, 22)
    def _(c):
        at = pl.multiple_of(c * ST, ST)
        v = pre1[pl.ds(at, ST), :]
        s = 1.0 / (1.0 + jnp.exp(-v))
        col = 16 * gx + c - 3
        ok = jnp.where((col >= 0) & (col < 512), 1.0, 0.0)
        h32[pl.ds(at + 8, ST), :] = v * s * (rows_ok_f * ok)
        sl1[pl.ds(at, ST), :] = s * (1.0 + v * (1.0 - s))

    shifts(h32, hs, 22 * ST)
    filter_end(1)
    for copy in cotcopies:
        copy.wait_recv()

    lane2 = lax.broadcasted_iota(jnp.int32, (CH, 256), 1)
    in_block = jnp.where(((lane2 & 63) >= 8) & ((lane2 & 63) < 56), 1.0, 0.0)
    for t in range(5):
        acc = None
        for j in range(3):
            term = mm(taps_in(1, j), hs[pl.ds(j * ST + t * 256, 256), :], NT)
            acc = term if acc is None else acc + term
        s = 1.0 / (1.0 + jnp.exp(-acc))
        act = (acc * s).astype(BF16).reshape(NGY, 32, 256)
        outer = cott[:, pl.ds(t * 256, 256)].astype(F32) * (s * (1.0 + acc * (1.0 - s)))
        if t == 0:
            outer = jnp.where((lane2 >= 128) | (gx > 0), outer, 0.0)
        if t == 4:
            outer = jnp.where((lane2 < 128) | (gx < NGX - 1), outer, 0.0)
        o32t[:, pl.ds(t * 256, 256)] = outer
        own = (outer * in_block).astype(BF16)
        lo, hi = (128 if t == 0 else 0), (128 if t == 4 else 256)
        outs[:, :, pl.ds(t * 256 + lo - 128, hi - lo)] = act[:, :, lo:hi]
        otb[:, pl.ds(t * 256 + lo - 128, hi - lo)] = own[:, lo:hi]

    def grad(g, left, right, base):
        copies = []
        for j in range(3):
            part = mm(left[...], right[pl.ds((base + j) * ST, 1024), :], NN)
            for i in range(3):
                value = part[:, i * CH:(i + 1) * CH].reshape(8, 2, 16, CH)
                gf[g, :, :, j * 3 + i] = value
                gb[g, :, :, j * 3 + i] = value.astype(BF16)
            taps = pl.ds(3 * j, 3)
            copies.append(go(rcopy(gb.at[g, :, 1 - core, taps], rb.at[g, :, taps], sp.at[g, j], rp.at[g, j], partner)))
        return copies

    def plane(g, pair):
        for copy in pair:
            copy.wait_recv()

        @pl.loop(0, NGY)
        def _(b):
            for k in range(2):
                lanes = pl.ds(k * 128, 128)
                part = gf[g, b, core, :, :, lanes] + rb[g, b, :, :, lanes].astype(F32)
                sb[g, b, k] = part.astype(BF16)

        copies = []
        for dx, dy in ((2, 2), (1, 2), (3, 2), (2, 1), (2, 3), (1, 1), (3, 3), (1, 3), (3, 1), (2, 0), (0, 2), (1, 0), (3, 0), (0, 1), (0, 3)):
            tx = lax.rem(x + dx, 4)
            dev = place(x + dx, y + dy, z, core)
            slot = dx * 4 + dy
            copies.append(
                go(rcopy(sb.at[g, dev["gy"], lax.div(tx, 2)], rx.at[g, slot], spl.at[g, slot], rpl.at[g, slot], dev))
            )
        return copies

    def scatter_copy(g, owner, source):
        return rcopy(tz.at[g, owner], rz.at[g, source], sz.at[g, owner], rzs.at[g, source], place(x, y, owner, core))

    def tail_scatter(g, copies):
        for copy in copies:
            copy.wait_recv()
        total = sb[g, gy, xh].astype(F32)
        for slot in range(1, 16):
            total = total + rx[g, slot].astype(F32)
        total = total.astype(BF16)
        for p in range(OWNERS):
            for n in range(2):
                tap = 2 * p + n
                tz[g, p, n] = total[tap] if tap < 9 else jnp.zeros((16, 128), BF16)
        for p in range(OWNERS):
            @pl.when(z != p)
            def _():
                scatter_copy(g, p, z).start()

    my_slot = z * 2 + xh

    def gather_copies(g):
        copies = []
        for dz in (4, 3, 5, 2, 6, 1, 7, 0):
            for dxh in (1, 0):
                if dz or dxh:
                    dev = place(x + 2 * dxh, y, z + dz, core)
                    ref = fin.at[g, my_slot]
                    copies.append(rcopy(ref, ref, sg.at[g, dz, dxh], rg.at[g, my_slot], dev))
        return copies

    def tail_gather(g):
        @pl.when(z < OWNERS)
        def _():
            for source in range(8):
                @pl.when(z != source)
                def _():
                    scatter_copy(g, z, source).wait_recv()
            rz[g, z] = tz[g, z]
            total = rz[g, 0].astype(F32)
            for source in range(1, 8):
                total = total + rz[g, source].astype(F32)
            fin[g, my_slot] = total.astype(BF16)
            for copy in gather_copies(g):
                copy.start()

    def tail_swap(g):
        for q in range(2 * OWNERS):
            @pl.when(my_slot != q)
            def _():
                ref = fin.at[g, q]
                rcopy(ref, ref, sg.at[g, 0, 0], rg.at[g, q], partner).wait_recv()
        return go(rcopy(fin.at[g], finp.at[g], sf.at[g], rf.at[g], partner))

    grads_o = (g1_o, g2_o)

    def tail_write(g, swap):
        for ref, half in ((fin, core), (finp, 1 - core)):
            if ref is finp:
                swap.wait_recv()
            rows = pl.ds(pl.multiple_of(16 * half, 16), 16)
            for q in range(2 * OWNERS):
                for n in range(2):
                    tap = 2 * (q // 2) + n
                    if tap < 9:
                        place_of = (tap % 3) * 3 + tap // 3
                        gv[g, place_of, rows, pl.ds((q % 2) * 128, 128)] = ref[g, q, n].astype(F32) * scale
        store = pltpu.make_async_copy(gv.at[g], grads_o[g], sout.at[2 + g])
        store.start()
        return store

    def tail_end(g):
        for p in range(OWNERS):
            @pl.when(z != p)
            def _():
                scatter_copy(g, p, z).wait_send()

        @pl.when(z < OWNERS)
        def _():
            for copy in gather_copies(g):
                copy.wait_send()

    pair2 = grad(1, otb, hs, 2)

    o32[pl.ds(0, 8), :] = jnp.zeros((8, CH), F32)
    o32[pl.ds(8 + 20 * ST, 8), :] = jnp.zeros((8, CH), F32)
    for t in range(5):
        o32[pl.ds(8 + t * 256, 256), :] = o32t[:, pl.ds(t * 256, 256)].T
    shifts(o32, os_, 20 * ST)

    plane2 = plane(1, pair2)

    i32[pl.ds(0, 8), :] = jnp.zeros((8, CH), F32)
    i32[pl.ds(8 + 18 * ST, 8), :] = jnp.zeros((8, CH), F32)
    for t in range(2):
        acc = None
        for j in range(3):
            term = mm(os_[pl.ds((2 - j) * ST + t * 576, 576), :], taps_out(1, j), NN)
            acc = term if acc is None else acc + term
        i32[pl.ds(8 + t * 576, 576), :] = acc

    @pl.loop(0, 18)
    def _(c):
        at = pl.multiple_of(c * ST, ST)
        col = 16 * gx + c - 1
        ok = jnp.where((col >= 0) & (col < 512), 1.0, 0.0)
        i32[pl.ds(at + 8, ST), :] = i32[pl.ds(at + 8, ST), :] * sl1[pl.ds(at + 128, ST), :] * (rows_ok_f * ok)

    for t in range(4):
        imt[:, pl.ds(t * 256, 256)] = (i32[pl.ds(8 + 64 + t * 256, 256), :].T * in_block).astype(BF16)
    pair1 = grad(0, imt, fs, 3)

    shifts(i32, is_, 18 * ST)
    plane1 = plane(0, pair1)
    outcopies = []
    for d in range(1, NGY):
        dev = at_gy(d)
        outcopies.append(go(rcopy(outs.at[dev["gy"]], rout.at[gy], so.at[d], ro.at[d], dev)))
    rout[gy] = outs[gy]

    acc = None
    for j in range(3):
        term = mm(is_[pl.ds((2 - j) * ST, 1024), :], taps_out(0, j), NN)
        acc = term if acc is None else acc + term
    for c in range(CB):
        put_strided(ig32, c, RB, CB, acc[c * ST + 8:c * ST + 8 + RB, :])
    igv[...] = joined(ig32).astype(BF16).reshape(RB, CB, CH)
    stores = [pltpu.make_async_copy(igv, ig_o, sout.at[0])]
    stores[0].start()

    tail_scatter(1, plane2)
    tail_gather(1)
    tail_scatter(0, plane1)

    for copy in outcopies:
        copy.wait_recv()
    rows_n = lax.broadcasted_iota(jnp.int32, (1024, 384), 0)
    h_lane = lax.broadcasted_iota(jnp.int32, (1, 384), 1)
    band = jnp.zeros((1, 384), jnp.int32)
    for b in range(1, NGY):
        band = band + jnp.where(h_lane >= 48 * b, 1, 0)
    for src in range(NGY):
        for cp in range(8):
            amat[pl.ds(cp * 32, 32), pl.ds(src * 128, 128)] = rout[src, :, pl.ds(cp * 128, 128)]
    for par in range(2):
        target = band * 80 + h_lane + (8 + 64 * par)
        sel2[...] = jnp.where(rows_n == target, 1.0, 0.0).astype(BF16)
        res = mm(amat[...], sel2[...], NN)
        for cp in range(8):
            put_strided(out32, 2 * cp + par, 32, CB, res[cp * 32:(cp + 1) * 32, :])
    outv[...] = joined(out32).astype(BF16).reshape(32, CB, 384)
    stores.append(pltpu.make_async_copy(outv, out_o, sout.at[1]))
    stores[1].start()

    tail_gather(0)
    swap2 = tail_swap(1)
    stores.append(tail_write(1, swap2))
    swap1 = tail_swap(0)
    stores.append(tail_write(0, swap1))

    for copy in pending:
        copy.wait_send()
    tail_end(1)
    tail_end(0)
    for store in stores:
        store.wait()


def solution(mesh):
    scale = 1.0 / math.sqrt(384 * 512)
    vm = pltpu.VMEM
    dma = pltpu.SemaphoreType.DMA
    scratch = [
        vm((RB, CB, CH), BF16),
        vm((9, 32, CH), BF16),
        vm((9, 32, CH), BF16),
        vm((32, CB, 384), BF16),
        vm((32, CB, 384), BF16),
        vm((RB, CB, CH), BF16),
        vm((2, 9, 32, CH), F32),
        vm((2, 768, 128), F32),
        vm((24 * ST + 16, CH), F32),
        vm((24 * ST, 768), BF16),
        vm((22 * ST, CH), F32),
        vm((22 * ST, CH), F32),
        vm((22 * ST + 16, CH), F32),
        vm((22 * ST, 768), BF16),
        vm((CH, 1280), BF16),
        vm((8, 32, 1024), BF16),
        vm((768, 128), BF16),
        vm((256, 768), BF16),
        vm((8, 32, 1024), BF16),
        vm((8, 32, 1024), BF16),
        vm((CH, 1024), BF16),
        vm((CH, 1280), F32),
        vm((20 * ST + 16, CH), F32),
        vm((20 * ST, 768), BF16),
        vm((18 * ST + 16, CH), F32),
        vm((CH, 1024), BF16),
        vm((18 * ST, 768), BF16),
        vm((2, 768, 128), F32),
        vm((256, 1024), BF16),
        vm((1024, 384), BF16),
        vm((3, 512, 128), F32),
        vm((2, 9, CH, CH), BF16),
        vm((2, 4, RB, CH), BF16),
        vm((2, 4, RB, CH), BF16),
        vm((2, 3, 4, 16, CH), BF16),
        vm((2, 3, 2, 64, 128), F32),
        vm((2, 8, 2, 9, 16, CH), F32),
        vm((2, 8, 2, 9, 16, CH), BF16),
        vm((2, 8, 9, 16, CH), BF16),
        vm((2, 8, 2, 9, 16, 128), BF16),
        vm((2, 16, 9, 16, 128), BF16),
        vm((2, OWNERS, 2, 16, 128), BF16),
        vm((2, 8, 2, 16, 128), BF16),
        vm((2, 2 * OWNERS, 2, 16, 128), BF16),
        vm((2, 2 * OWNERS, 2, 16, 128), BF16),
        dma((2, 3)), dma((2, 3)),
        dma((2, 4, 2)), dma((2, 4, 2)),
        dma((2, 2, 4)), dma((2, 2, 4)),
        dma((3, 3)), dma((3, 3)),
        dma((3, 8)), dma((3, 8)),
        dma((8,)), dma((8,)),
        dma((2, 3)), dma((2, 3)),
        dma((2, 16)), dma((2, 16)),
        dma((2, OWNERS)), dma((2, 8)),
        dma((2, 8, 2)), dma((2, 2 * OWNERS)),
        dma((2,)), dma((2,)),
        dma((4,)), dma((4,)),
    ]
    call = pl.pallas_call(
        functools.partial(kernel, scale),
        name="step",
        out_shape=(
            jax.ShapeDtypeStruct((32, CB, 384), BF16),
            jax.ShapeDtypeStruct((RB, CB, CH), BF16),
            jax.ShapeDtypeStruct((9, 32, CH), F32),
            jax.ShapeDtypeStruct((9, 32, CH), F32),
        ),
        in_specs=[pl.BlockSpec(memory_space=pl.ANY)] * 4,
        out_specs=[pl.BlockSpec(memory_space=pl.ANY)] * 4,
        scratch_shapes=scratch,
        compiler_params=pltpu.CompilerParams(
            collective_id=0, has_side_effects=True, vmem_limit_bytes=60 * 1024 * 1024
        ),
    )

    def taps_first(shard):
        return jnp.transpose(shard, (1, 2, 0, 3)).reshape(9, 32, CH)

    def taps_inside(grad):
        return jnp.transpose(grad.reshape(3, 3, 32, CH), (2, 0, 1, 3))

    def body(features, first_filter, second_filter, cotangent):
        out, ig, g1, g2 = call(features, taps_first(first_filter), taps_first(second_filter), cotangent)
        return out, ig, taps_inside(g1), taps_inside(g2)

    in_specs = (
        P("gy", "gx", None),
        P("gy", None, None, None),
        P("gy", None, None, None),
        P("gy", "gx", None),
    )
    out_specs = (
        P("gy", "gx", None),
        P("gy", "gx", None),
        P("gy", None, None, None),
        P("gy", None, None, None),
    )
    return jax.shard_map(body, mesh=mesh, in_specs=in_specs, out_specs=out_specs, check_vma=False)
```
